32 devices in a mesh: row: 2 (over x), col: 16 (over z, y, core).
Axes of the slice: x: 2, y: 2, z: 4, core: 2. Of those that a mesh axis runs over, the one named last changes fastest.
Arguments:
- query_proj: bfloat16 [16384, 4096], P(('col', 'row')), may hold values from -9 to 9
- key_proj: bfloat16 [16384, 512], P(('col', 'row')), may hold values from -9 to 9
- value_proj: bfloat16 [16384, 512], P(('col', 'row')), may hold values from -6 to 6
- segment_ids: int32 [16, 1024], P('col'), may hold values from 0 to 3, never falling along the last dimension, each value on 1 to 512 neighbouring positions
- out_weight: bfloat16 [4096, 8192], P('col', 'row'), may hold values from -0.09375 to 0.09375
- residual: bfloat16 [16384, 8192], P('col', 'row'), may hold values from -4 to 4
- norm_gain: float32 [8192], P('row'), may hold values from 0.1 to 1.9
Outputs:
- residual_sum: bfloat16 [16384, 8192], P('col', 'row')
- normed: bfloat16 [16384, 8192], P('col', 'row')
The draws below stay inside these ranges and needn't reach their ends.
Inputs may be any that keep to these rules, and one draw needn't show every extreme that they name: `segment_ids`: along each packed sequence the document number never falls; each document spans at most 512 positions and one spans exactly that.
All inputs are finite; a program needn't handle non-finite values.
Results may differ from the reference program's by a relative error of at most 0.0044.
Values may be sent and summed in bfloat16 or wider, within the bound.
A program may use at most 192 MiB of HBM per device.

```python
import math
import jax
import jax.numpy as jnp
import numpy as np
from jax import lax

D = 8192
HD = 128
HQ = 32
HK = 4
SEQ = 1024
QW = 4096
PACKS = 16
TOKENS = 16384


def shared_keys(key):
    width = HK * HD
    base_keys = jnp.clip(jax.random.normal(jax.random.fold_in(key, 11), (TOKENS, width), jnp.float32), -4.0, 4.0)
    keys_out = base_keys
    return keys_out


def draw_key_proj(key, part):
    keys_out = shared_keys(key)
    return keys_out.astype(jnp.bfloat16)


def draw_query_proj(key, part):
    query_out = jnp.clip(jax.random.normal(jax.random.fold_in(key, 21), (TOKENS, HQ * HD), jnp.float32), -4.0, 4.0)
    return query_out.astype(jnp.bfloat16)


def block_levels(stream_key, shape, split, low, largest):
    factor_of, own = 1.0, jax.random.fold_in(stream_key, 6)
    for axis_at, parts in split:
        steps = jnp.exp(jax.random.uniform(jax.random.fold_in(own, axis_at), (parts,), jnp.float32, low / len(split), largest / len(split)))
        factor_of = factor_of * jnp.repeat(steps, shape[axis_at] // parts).reshape([-1 if axis == axis_at else 1 for axis in range(len(shape))])
    return factor_of


def length_profile(amount, total, limit, skew):
    weights = [(1 << 20) // math.isqrt(grade ** skew) + 1 for grade in range(2, amount + 1)]
    rest, given = total - limit - (amount - 1), [1] * (amount - 1)
    while rest > 0:
        free = [i for i in range(amount - 1) if given[i] < limit]
        pool, remaining = sum([weights[i] for i in free]), rest
        for i in free:
            extra = min(limit - given[i], max(1, remaining * weights[i] // pool), rest)
            given[i] = given[i] + extra
            rest = rest - extra
    return np.array([limit] + given)


def ragged_sizes(key, number_of, total, reach, slope):
    if number_of == 2:
        one = jax.random.randint(key, (), max(1, total - reach), min(reach, total - 1) + 1)
        return jnp.stack([one, total - one])
    sizes = jnp.asarray(length_profile(number_of, total, reach, slope), jnp.int32)
    couples = (number_of - 1) // 2
    donor, receiver = sizes[1:1 + 2 * couples:2], sizes[2:2 + 2 * couples:2]
    slack = jnp.minimum(donor - 1, reach - receiver)
    moved = jax.random.randint(jax.random.fold_in(key, 1), (couples,), 0, 1 << 20) % (slack + 1)
    sizes = sizes.at[1:1 + 2 * couples:2].set(donor - moved).at[2:2 + 2 * couples:2].set(receiver + moved)
    return sizes[jax.random.permutation(jax.random.fold_in(key, 2), number_of)]


def noise(rng, dims, scale, limit, pieces=(), held_as=jnp.bfloat16):
    values = scale * jax.random.normal(rng, dims, jnp.float32)
    if pieces:
        values = values * block_levels(rng, dims, pieces, -0.22, 0.18)
    return jnp.clip(values, -limit, limit).astype(held_as)


def setup_inputs(seed: int = 0) -> dict:
    keys = jax.random.split(jax.random.key(seed), 8)
    query_proj = draw_query_proj(jax.random.fold_in(keys[7], 71), 0)
    key_proj = draw_key_proj(jax.random.fold_in(keys[7], 71), 0)
    value_proj = noise(keys[2], (TOKENS, HK * HD), 1.0, 6.0, ((0, 32),))
    segment_ids = jax.vmap(lambda own: jnp.searchsorted(jnp.cumsum(ragged_sizes(own, 4, SEQ, SEQ // 2, 0)), jnp.arange(SEQ), side="right"))(jax.random.split(keys[3], PACKS)).reshape((PACKS, SEQ)).astype(jnp.int32)
    out_weight = noise(keys[4], (QW, D), QW ** -0.5, 0.09375, ((0, 16), (1, 2)))
    residual = noise(keys[5], (TOKENS, D), 0.25, 4.0, ((0, 16), (1, 2)))
    norm_gain = jnp.clip(1.0 + 0.18 * jax.random.normal(keys[6], (D,), jnp.float32), 0.1, 1.9)
    return {"query_proj": query_proj, "key_proj": key_proj, "value_proj": value_proj, "segment_ids": segment_ids, "out_weight": out_weight, "residual": residual, "norm_gain": norm_gain}


def attend_pack(operands):
    query_rows, key_rows, value_rows, segment_row = operands
    group = HQ // HK
    query_grid = query_rows.reshape(SEQ, HK, group, HD).transpose(1, 2, 0, 3).astype(jnp.float32)
    key_grid = key_rows.reshape(SEQ, HK, HD).transpose(1, 0, 2).astype(jnp.float32)
    value_grid = value_rows.reshape(SEQ, HK, HD).transpose(1, 0, 2).astype(jnp.float32)
    places = jnp.arange(SEQ)
    allowed = (segment_row[:, None] == segment_row[None, :]) & (places[None, :] <= places[:, None])
    scores = jnp.einsum('hgqd,hkd->hgqk', query_grid, key_grid) * HD ** (-0.5)
    scores = jnp.where(allowed, scores, jnp.float32(-1e+30))
    peak = lax.optimization_barrier(jnp.max(scores, axis=-1, keepdims=True))
    weights = jnp.where(allowed, jnp.exp(scores - peak), jnp.float32(0.0))
    totals = lax.optimization_barrier(jnp.sum(weights, axis=-1, keepdims=True))
    probs = lax.optimization_barrier(weights.astype(jnp.bfloat16))
    mixture = jnp.einsum('hgqk,hkd->hgqd', probs.astype(jnp.float32), value_grid) / totals
    mixture = mixture.astype(jnp.bfloat16)
    return mixture.transpose(2, 0, 1, 3).reshape(SEQ, HQ * HD)

def reference(query_proj, key_proj, value_proj, segment_ids, out_weight, residual, norm_gain):
    packs = segment_ids.shape[0]
    query_all = query_proj.reshape(packs, SEQ, HQ * HD)
    key_all = key_proj.reshape(packs, SEQ, HK * HD)
    value_all = value_proj.reshape(packs, SEQ, HK * HD)
    attn = lax.map(attend_pack, (query_all, key_all, value_all, segment_ids))
    attn = attn.reshape(packs * SEQ, HQ * HD)
    projected = jnp.dot(attn, out_weight, preferred_element_type=jnp.float32)
    hidden_sum = residual.astype(jnp.float32) + projected
    mean_square = lax.optimization_barrier(jnp.mean(hidden_sum * hidden_sum, axis=1))
    scaled = lax.rsqrt(mean_square + jnp.float32(1e-05))
    normed = hidden_sum * scaled[:, None] * norm_gain[None, :]
    return (hidden_sum.astype(jnp.bfloat16), normed.astype(jnp.bfloat16))
```

```python
import functools
import math

import jax
import jax.numpy as jnp
from jax import lax
from jax.experimental import pallas as pl
from jax.experimental.pallas import tpu as pltpu
from jax.sharding import PartitionSpec as P

D = 8192
HD = 128
HK = 4
MESH = pl.DeviceIdType.MESH


def attend_local(query_heads, key_heads, value_heads, segment_row):
    length = query_heads.shape[0]
    kv_local = key_heads.shape[1] // HD
    group = query_heads.shape[1] // HD // kv_local
    query_grid = query_heads.reshape(length, kv_local, group, HD).transpose(1, 2, 0, 3)
    key_grid = key_heads.reshape(length, kv_local, HD).transpose(1, 0, 2)
    value_grid = value_heads.reshape(length, kv_local, HD).transpose(1, 0, 2)
    places = jnp.arange(length)
    allowed = (segment_row[:, None] == segment_row[None, :]) & (places[None, :] <= places[:, None])

    def one_group(operands):
        group_query, group_key, group_value = operands
        scores = jnp.einsum(
            "gqd,kd->gqk", group_query, group_key, preferred_element_type=jnp.float32
        ) * HD ** (-0.5)
        scores = jnp.where(allowed, scores, jnp.float32(-1e30))
        peak = jnp.max(scores, axis=-1, keepdims=True)
        weights = jnp.where(allowed, jnp.exp(scores - peak), jnp.float32(0.0))
        totals = jnp.sum(weights, axis=-1, keepdims=True)
        probs = weights.astype(jnp.bfloat16)
        mixture = (
            jnp.einsum("gqk,kd->gqd", probs, group_value, preferred_element_type=jnp.float32)
            / totals
        )
        return mixture.astype(jnp.bfloat16)

    heads_out = lax.map(one_group, (query_grid, key_grid, value_grid))
    return heads_out.transpose(2, 0, 1, 3).reshape(length, kv_local * group * HD)


def widen_heads(proj_rows, repeat):
    rows_local = proj_rows.shape[0]
    kv_count = proj_rows.shape[1] // HD
    if repeat == 1:
        return proj_rows
    spread = jnp.broadcast_to(
        proj_rows.reshape(rows_local, kv_count, 1, HD), (rows_local, kv_count, repeat, HD)
    )
    return spread.reshape(rows_local, kv_count * repeat * HD)


def body_any(query_proj, key_proj, value_proj, segment_ids, out_weight, residual, norm_gain):
    row_count = lax.axis_size("row")
    repeat = max(row_count // HK, 1)
    key_wide = widen_heads(key_proj, repeat)
    value_wide = widen_heads(value_proj, repeat)
    query_heads, key_heads, value_heads = (
        lax.all_to_all(query_proj, "row", split_axis=1, concat_axis=0, tiled=True),
        lax.all_to_all(key_wide, "row", split_axis=1, concat_axis=0, tiled=True),
        lax.all_to_all(value_wide, "row", split_axis=1, concat_axis=0, tiled=True),
    )
    attn = attend_local(query_heads, key_heads, value_heads, segment_ids[0])
    panel_rows = lax.all_gather(attn, "row", axis=1, tiled=True)
    projected = jnp.dot(
        panel_rows,
        lax.all_gather(out_weight, "col", axis=0, tiled=True),
        preferred_element_type=jnp.float32,
    )
    hidden_sum = residual.astype(jnp.float32) + projected
    squares = lax.psum(jnp.sum(hidden_sum * hidden_sum, axis=1), "row")
    scaled = lax.rsqrt(squares / D + jnp.float32(1e-05))
    normed = hidden_sum * scaled[:, None] * norm_gain[None, :]
    return (hidden_sum.astype(jnp.bfloat16), normed.astype(jnp.bfloat16))


NZ = 4
CH = 4
QT = 256
KT = 768
STEPS = 8
NB = 512


def fused_kernel(q_ref, k_ref, v_ref, seg_row, seg_col, w_ref, res_ref,
                 hid_ref, sq_ref, wfull,
                 qbuf, kbuf, vbuf, bias, attn, wbuf, obuf, acc, sqbuf,
                 send, recv, loc, lw, a_send, a_recv, x_send, x_recv, osem):
    r = lax.axis_index("row")
    col = lax.axis_index("col")
    core = lax.rem(col, 2)
    y = lax.rem(col // 2, 2)
    z = col // 4
    half = q_ref.shape[0]
    wrows = w_ref.shape[0]
    crow = wrows // CH
    width = w_ref.shape[1]

    def cid(zz, yy, cc):
        return (zz * 2 + yy) * 2 + cc

    right = (r, cid(z + 1, y, core))
    left = (r, cid(z - 1, y, core))
    across = (r, cid(z, 1 - y, core))
    sibling = (r, cid(z, y, 1 - core))
    partner = (1 - r, col)

    barrier = pltpu.get_barrier_semaphore()

    def greet(dev):
        pl.semaphore_signal(barrier, inc=1, device_id=dev, device_id_type=MESH)

    greet(across)
    greet(sibling)
    greet(partner)

    @pl.when(z > 0)
    def _():
        greet(left)

    @pl.when(z < NZ - 1)
    def _():
        greet(right)

    at_end = (z == 0) | (z == NZ - 1)

    @pl.when(at_end)
    def _():
        pl.semaphore_wait(barrier, 4)

    @pl.when(jnp.logical_not(at_end))
    def _():
        pl.semaphore_wait(barrier, 5)

    def wcopy(way, dev, zz, yy, j, own):
        slot = cid(zz, yy, core)
        rows = pl.ds(j * crow, crow)
        src = w_ref.at[rows, :] if own else wfull.at[slot, rows, :]
        return pltpu.make_async_remote_copy(
            src_ref=src, dst_ref=wfull.at[slot, rows, :],
            send_sem=send.at[way, zz * 2 + yy, j], recv_sem=recv.at[slot, j],
            device_id=dev, device_id_type=MESH)

    def wait_chunk(slot, j):
        rows = pl.ds(j * crow, crow)
        pltpu.make_async_copy(wfull.at[slot, rows, :], wfull.at[slot, rows, :], recv.at[slot, j]).wait()

    own_w = pltpu.make_async_copy(w_ref, wfull.at[col], loc.at[0])
    k_local = pltpu.make_async_copy(k_ref, kbuf.at[pl.ds(r * half, half), :], loc.at[1])
    v_local = pltpu.make_async_copy(v_ref, vbuf.at[pl.ds(r * half, half), :], loc.at[2])
    q_local = pltpu.make_async_copy(q_ref, qbuf, loc.at[3])
    res_local = pltpu.make_async_copy(res_ref, obuf, loc.at[4])

    def kv_remote(src, dst, i):
        return pltpu.make_async_remote_copy(
            src_ref=src, dst_ref=dst.at[pl.ds(r * half, half), :],
            send_sem=x_send.at[i], recv_sem=x_recv.at[i],
            device_id=partner, device_id_type=MESH)

    k_rem = kv_remote(k_ref, kbuf, 0)
    v_rem = kv_remote(v_ref, vbuf, 1)
    k_rem.start()
    v_rem.start()
    for j in range(CH):
        @pl.when(z < NZ - 1)
        def _():
            wcopy(0, right, z, y, j, True).start()

        @pl.when(z > 0)
        def _():
            wcopy(1, left, z, y, j, True).start()

        wcopy(2, across, z, y, j, True).start()
    k_local.start()
    v_local.start()
    q_local.start()
    res_local.start()
    own_w.start()
    for j in range(CH):
        wcopy(3, sibling, z, y, j, True).start()

    scale = HD ** (-0.5) * math.log2(math.e)
    starts = []
    for i in range(half // QT):
        t0 = pl.multiple_of(r * half + i * QT, QT)
        ks = pl.multiple_of(jnp.maximum(t0 + QT - KT, 0), QT)
        starts.append((t0, ks))
        qs = seg_col[pl.ds(t0, QT), :]
        ksg = seg_row[:, pl.ds(ks, KT)]
        qp = t0 + lax.broadcasted_iota(jnp.int32, (QT, KT), 0)
        kp = ks + lax.broadcasted_iota(jnp.int32, (QT, KT), 1)
        keep = (qs == ksg) & (kp <= qp)
        bias[i] = jnp.where(keep, jnp.float32(0.0), jnp.float32(-1e30))

    q_local.wait()
    k_local.wait()
    v_local.wait()
    k_rem.wait_recv()
    v_rem.wait_recv()

    heads = qbuf.shape[1] // HD
    per_step = heads // STEPS
    aw = per_step * HD
    group = heads // HK

    def attn_copy(g):
        cols = pl.ds(pl.multiple_of(g * aw, aw), aw)
        part = attn.at[pl.ds(pl.multiple_of(r * half, half), half), cols]
        return pltpu.make_async_remote_copy(
            src_ref=part, dst_ref=part, send_sem=a_send.at[g], recv_sem=a_recv.at[g],
            device_id=partner, device_id_type=MESH)

    @pl.loop(0, STEPS)
    def _(g):
        kcol = pl.ds(pl.multiple_of((g * per_step // group) * HD, HD), HD)
        for i, (t0, ks) in enumerate(starts):
            key = kbuf[pl.ds(ks, KT), kcol]
            val = vbuf[pl.ds(ks, KT), kcol]
            for h in range(per_step):
                hc = pl.ds(pl.multiple_of(g * aw + h * HD, HD), HD)
                qh = qbuf[i * QT:(i + 1) * QT, hc]
                s = lax.dot_general(qh, key, (((1,), (1,)), ((), ())),
                                    preferred_element_type=jnp.float32)
                s = s * scale + bias[i]
                m = jnp.max(s, axis=1, keepdims=True)
                p = jnp.exp2(s - m)
                tot = jnp.sum(p, axis=1, keepdims=True)
                o = jnp.dot(p.astype(jnp.bfloat16), val, preferred_element_type=jnp.float32)
                attn[pl.ds(t0, QT), hc] = (o / tot).astype(jnp.bfloat16)
        attn_copy(g).start()

    def place(t):
        h = (t + 1) // 2
        return z - h if t % 2 == 1 else z + h

    def guard(t, f):
        if t == 0:
            f()
        elif t % 2 == 1:
            pl.when(place(t) >= 0)(f)
        else:
            pl.when(place(t) < NZ)(f)

    def forward(t):
        def go():
            zz = place(t)

            @pl.loop(0, CH)
            def _(j):
                wait_chunk(cid(zz, y, core), j)
                if t % 2 == 1:
                    @pl.when(z < NZ - 1)
                    def _():
                        wcopy(0, right, zz, y, j, False).start()
                else:
                    @pl.when(z > 0)
                    def _():
                        wcopy(1, left, zz, y, j, False).start()
                wcopy(2, across, zz, y, j, False).start()
                wcopy(3, sibling, zz, y, j, False).start()
        guard(t, go)

    def forward_y(t):
        def go():
            zz = place(t)

            @pl.loop(0, CH)
            def _(j):
                wait_chunk(cid(zz, 1 - y, core), j)
                wcopy(3, sibling, zz, 1 - y, j, False).start()
        guard(t, go)

    nsteps = width // NB

    def project(t, yy):
        def go():
            zz = place(t)

            @pl.loop(0, CH)
            def _(j):
                wait_chunk(cid(zz, yy, 1 - core), j)

            first = cid(zz, yy, 0)

            def wload(n, c):
                cols = pl.ds(pl.multiple_of(n * NB, NB), NB)
                return pltpu.make_async_copy(
                    wfull.at[first + c, :, cols], wbuf.at[pl.ds(c * wrows, wrows), cols],
                    lw.at[c, n])

            @pl.loop(0, nsteps)
            def _(n):
                wload(n, 0).start()
                wload(n, 1).start()

            kc = pl.ds(pl.multiple_of(first * wrows, 2 * wrows), 2 * wrows)

            @pl.loop(0, nsteps)
            def _(n):
                cols = pl.ds(pl.multiple_of(n * NB, NB), NB)
                wload(n, 0).wait()
                wload(n, 1).wait()
                acc[:, cols] += jnp.dot(attn[:, kc], wbuf[:, cols],
                                        preferred_element_type=jnp.float32)
        guard(t, go)

    forward(1)
    forward(2)
    res_local.wait()

    @pl.loop(0, nsteps)
    def _(n):
        cols = pl.ds(pl.multiple_of(n * NB, NB), NB)
        acc[:, cols] = obuf[:, cols].astype(jnp.float32)

    own_w.wait()
    forward_y(0)
    forward(3)
    forward(4)

    @pl.loop(0, STEPS)
    def _(g):
        attn_copy(g).wait_send()
        cols = pl.ds(pl.multiple_of(g * aw, aw), aw)
        part = attn.at[pl.ds(pl.multiple_of((1 - r) * half, half), half), cols]
        pltpu.make_async_copy(part, part, a_recv.at[g]).wait()

    project(0, y)
    project(1, y)
    project(2, y)
    forward(5)
    forward(6)
    project(0, 1 - y)
    forward_y(1)
    forward_y(2)
    project(3, y)
    project(4, y)
    project(1, 1 - y)
    project(2, 1 - y)
    forward_y(3)
    forward_y(4)
    project(5, y)
    project(6, y)
    project(3, 1 - y)
    project(4, 1 - y)
    forward_y(5)
    forward_y(6)
    project(5, 1 - y)
    project(6, 1 - y)

    def out_copy(n):
        cols = pl.ds(pl.multiple_of(n * NB, NB), NB)
        return pltpu.make_async_copy(obuf.at[:, cols], hid_ref.at[:, cols], osem.at[n])

    def finish(n, part):
        cols = pl.ds(pl.multiple_of(n * NB, NB), NB)
        a = acc[:, cols]
        obuf[:, cols] = a.astype(jnp.bfloat16)
        out_copy(n).start()
        sqr = a * a
        for i in range(NB // 128):
            part = part + sqr[:, i * 128:(i + 1) * 128]
        return part

    part = lax.fori_loop(0, nsteps, finish, jnp.zeros((acc.shape[0], 128), jnp.float32))
    sqbuf[0] = jnp.sum(part.T, axis=0, keepdims=True)
    x_sq = pltpu.make_async_remote_copy(
        src_ref=sqbuf.at[0], dst_ref=sqbuf.at[1], send_sem=x_send.at[2], recv_sem=x_recv.at[2],
        device_id=partner, device_id_type=MESH)
    x_sq.start()

    k_rem.wait_send()
    v_rem.wait_send()
    for t in range(2 * NZ - 1):
        def sent(t=t):
            zz = place(t)

            @pl.loop(0, CH)
            def _(j):
                if t % 2 == 1 or t == 0:
                    @pl.when(z < NZ - 1)
                    def _():
                        wcopy(0, right, zz, y, j, False).wait_send()
                if t % 2 == 0:
                    @pl.when(z > 0)
                    def _():
                        wcopy(1, left, zz, y, j, False).wait_send()
                wcopy(2, across, zz, y, j, False).wait_send()
                wcopy(3, sibling, zz, y, j, False).wait_send()
                wcopy(3, sibling, zz, 1 - y, j, False).wait_send()
        guard(t, sent)

    @pl.loop(0, nsteps)
    def _(n):
        out_copy(n).wait()

    x_sq.wait()
    sq_ref[...] = sqbuf[0] + sqbuf[1]


def body_fused(query_proj, key_proj, value_proj, segment_ids, out_weight, residual, norm_gain):
    half, qw = query_proj.shape
    length = segment_ids.shape[1]
    wrows, width = out_weight.shape
    cols = lax.axis_size("col")
    hbm = pl.BlockSpec(memory_space=pl.ANY)
    vmem = pl.BlockSpec(memory_space=pltpu.VMEM)
    dma = pltpu.SemaphoreType.DMA
    hidden, squares, _ = pl.pallas_call(
        fused_kernel,
        out_shape=(
            jax.ShapeDtypeStruct((length, width), jnp.bfloat16),
            jax.ShapeDtypeStruct((1, length), jnp.float32),
            jax.ShapeDtypeStruct((cols, wrows, width), jnp.bfloat16),
        ),
        in_specs=[hbm, hbm, hbm, vmem, vmem, hbm, hbm],
        out_specs=(hbm, vmem, hbm),
        scratch_shapes=[
            pltpu.VMEM((half, qw), jnp.bfloat16),
            pltpu.VMEM((length, HK * HD), jnp.bfloat16),
            pltpu.VMEM((length, HK * HD), jnp.bfloat16),
            pltpu.VMEM((half // QT, QT, KT), jnp.float32),
            pltpu.VMEM((length, qw), jnp.bfloat16),
            pltpu.VMEM((2 * wrows, width), jnp.bfloat16),
            pltpu.VMEM((length, width), jnp.bfloat16),
            pltpu.VMEM((length, width), jnp.float32),
            pltpu.VMEM((2, 1, length), jnp.float32),
            dma((4, cols // 2, CH)),
            dma((cols, CH)),
            dma((5,)),
            dma((2, width // NB)),
            dma((STEPS,)),
            dma((STEPS,)),
            dma((3,)),
            dma((3,)),
            dma((width // NB,)),
        ],
        compiler_params=pltpu.CompilerParams(
            collective_id=0, has_side_effects=True, vmem_limit_bytes=60 * 1024 * 1024),
        name="fused",
    )(query_proj, key_proj, value_proj, segment_ids, segment_ids.reshape(length, 1),
      out_weight, residual)
    scaled = lax.rsqrt(squares[0] / D + jnp.float32(1e-05))
    normed = hidden.astype(jnp.float32) * scaled[:, None] * norm_gain[None, :]
    return hidden, normed.astype(jnp.bfloat16)


def solution(mesh):
    placed = (
        P(("col", "row"), None),
        P(("col", "row"), None),
        P(("col", "row"), None),
        P("col", None),
        P("col", "row"),
        P("col", "row"),
        P("row"),
    )
    known = mesh.shape["row"] == 2 and mesh.shape["col"] == 4 * NZ
    return jax.shard_map(
        body_fused if known else body_any,
        mesh=mesh,
        in_specs=placed,
        out_specs=(P("col", "row"), P("col", "row")),
        check_vma=False,
    )
```

```python
import functools
import math

import jax
import jax.numpy as jnp
from jax import lax
from jax.experimental import pallas as pl
from jax.experimental.pallas import tpu as pltpu
from jax.sharding import PartitionSpec as P

D = 8192
HD = 128
HK = 4
MESH = pl.DeviceIdType.MESH


def attend_local(query_heads, key_heads, value_heads, segment_row):
    length = query_heads.shape[0]
    kv_local = key_heads.shape[1] // HD
    group = query_heads.shape[1] // HD // kv_local
    query_grid = query_heads.reshape(length, kv_local, group, HD).transpose(1, 2, 0, 3)
    key_grid = key_heads.reshape(length, kv_local, HD).transpose(1, 0, 2)
    value_grid = value_heads.reshape(length, kv_local, HD).transpose(1, 0, 2)
    places = jnp.arange(length)
    allowed = (segment_row[:, None] == segment_row[None, :]) & (places[None, :] <= places[:, None])

    def one_group(operands):
        group_query, group_key, group_value = operands
        scores = jnp.einsum(
            "gqd,kd->gqk", group_query, group_key, preferred_element_type=jnp.float32
        ) * HD ** (-0.5)
        scores = jnp.where(allowed, scores, jnp.float32(-1e30))
        peak = jnp.max(scores, axis=-1, keepdims=True)
        weights = jnp.where(allowed, jnp.exp(scores - peak), jnp.float32(0.0))
        totals = jnp.sum(weights, axis=-1, keepdims=True)
        probs = weights.astype(jnp.bfloat16)
        mixture = (
            jnp.einsum("gqk,kd->gqd", probs, group_value, preferred_element_type=jnp.float32)
            / totals
        )
        return mixture.astype(jnp.bfloat16)

    heads_out = lax.map(one_group, (query_grid, key_grid, value_grid))
    return heads_out.transpose(2, 0, 1, 3).reshape(length, kv_local * group * HD)


def widen_heads(proj_rows, repeat):
    rows_local = proj_rows.shape[0]
    kv_count = proj_rows.shape[1] // HD
    if repeat == 1:
        return proj_rows
    spread = jnp.broadcast_to(
        proj_rows.reshape(rows_local, kv_count, 1, HD), (rows_local, kv_count, repeat, HD)
    )
    return spread.reshape(rows_local, kv_count * repeat * HD)


def body_any(query_proj, key_proj, value_proj, segment_ids, out_weight, residual, norm_gain):
    row_count = lax.axis_size("row")
    repeat = max(row_count // HK, 1)
    key_wide = widen_heads(key_proj, repeat)
    value_wide = widen_heads(value_proj, repeat)
    query_heads, key_heads, value_heads = (
        lax.all_to_all(query_proj, "row", split_axis=1, concat_axis=0, tiled=True),
        lax.all_to_all(key_wide, "row", split_axis=1, concat_axis=0, tiled=True),
        lax.all_to_all(value_wide, "row", split_axis=1, concat_axis=0, tiled=True),
    )
    attn = attend_local(query_heads, key_heads, value_heads, segment_ids[0])
    panel_rows = lax.all_gather(attn, "row", axis=1, tiled=True)
    projected = jnp.dot(
        panel_rows,
        lax.all_gather(out_weight, "col", axis=0, tiled=True),
        preferred_element_type=jnp.float32,
    )
    hidden_sum = residual.astype(jnp.float32) + projected
    squares = lax.psum(jnp.sum(hidden_sum * hidden_sum, axis=1), "row")
    scaled = lax.rsqrt(squares / D + jnp.float32(1e-05))
    normed = hidden_sum * scaled[:, None] * norm_gain[None, :]
    return (hidden_sum.astype(jnp.bfloat16), normed.astype(jnp.bfloat16))


NZ = 4
CH = 8
QT = 256
KT = 768
STEPS = 8
NB = 512


def fused_kernel(q_ref, k_ref, v_ref, seg_row, w_ref, res_ref,
                 hid_ref, sq_ref, wfull,
                 qbuf, kbuf, vbuf, bias, attn, wbuf, obuf, acc, sqbuf,
                 send, recv, loc, lw, a_send, a_recv, x_send, x_recv, osem):
    r = lax.axis_index("row")
    col = lax.axis_index("col")
    core = lax.rem(col, 2)
    y = lax.rem(col // 2, 2)
    z = col // 4
    half = q_ref.shape[0]
    wrows = w_ref.shape[0]
    crow = wrows // CH
    width = w_ref.shape[1]

    def cid(zz, yy, cc):
        return (zz * 2 + yy) * 2 + cc

    right = (r, cid(z + 1, y, core))
    left = (r, cid(z - 1, y, core))
    across = (r, cid(z, 1 - y, core))
    sibling = (r, cid(z, y, 1 - core))
    partner = (1 - r, col)

    barrier = pltpu.get_barrier_semaphore()

    def greet(dev):
        pl.semaphore_signal(barrier, inc=1, device_id=dev, device_id_type=MESH)

    greet(across)
    greet(sibling)
    greet(partner)

    @pl.when(z > 0)
    def _():
        greet(left)

    @pl.when(z < NZ - 1)
    def _():
        greet(right)

    at_end = (z == 0) | (z == NZ - 1)

    @pl.when(at_end)
    def _():
        pl.semaphore_wait(barrier, 4)

    @pl.when(jnp.logical_not(at_end))
    def _():
        pl.semaphore_wait(barrier, 5)

    def wcopy(way, dev, zz, yy, j, own):
        slot = cid(zz, yy, core)
        rows = pl.ds(j * crow, crow)
        src = w_ref.at[rows, :] if own else wfull.at[slot, rows, :]
        return pltpu.make_async_remote_copy(
            src_ref=src, dst_ref=wfull.at[slot, rows, :],
            send_sem=send.at[way, zz * 2 + yy, j], recv_sem=recv.at[slot, j],
            device_id=dev, device_id_type=MESH)

    def wait_chunk(slot, j):
        rows = pl.ds(j * crow, crow)
        pltpu.make_async_copy(wfull.at[slot, rows, :], wfull.at[slot, rows, :], recv.at[slot, j]).wait()

    own_w = pltpu.make_async_copy(w_ref, wfull.at[col], loc.at[0])
    k_local = pltpu.make_async_copy(k_ref, kbuf.at[pl.ds(r * half, half), :], loc.at[1])
    v_local = pltpu.make_async_copy(v_ref, vbuf.at[pl.ds(r * half, half), :], loc.at[2])
    q_local = pltpu.make_async_copy(q_ref, qbuf, loc.at[3])
    res_local = pltpu.make_async_copy(res_ref, obuf, loc.at[4])

    def kv_remote(src, dst, i):
        return pltpu.make_async_remote_copy(
            src_ref=src, dst_ref=dst.at[pl.ds(r * half, half), :],
            send_sem=x_send.at[i], recv_sem=x_recv.at[i],
            device_id=partner, device_id_type=MESH)

    k_rem = kv_remote(k_ref, kbuf, 0)
    v_rem = kv_remote(v_ref, vbuf, 1)
    k_rem.start()
    v_rem.start()
    wcopy(2, across, z, y, CH - 1, True).start()
    for j in range(CH):
        @pl.when(z < NZ - 1)
        def _():
            wcopy(0, right, z, y, j, True).start()

        @pl.when(z > 0)
        def _():
            wcopy(1, left, z, y, j, True).start()

        if j < CH - 1:
            wcopy(2, across, z, y, j, True).start()
    k_local.start()
    v_local.start()
    q_local.start()
    res_local.start()
    own_w.start()
    for j in range(CH):
        wcopy(3, sibling, z, y, j, True).start()

    def place(t):
        h = (t + 1) // 2
        return z - h if t % 2 == 1 else z + h

    def guard(t, f):
        if t == 0:
            f()
        elif t % 2 == 1:
            pl.when(place(t) >= 0)(f)
        else:
            pl.when(place(t) < NZ)(f)

    def on_z(t, yy, j, act):
        zz = place(t)
        if t % 2 == 1 or t == 0:
            @pl.when(z < NZ - 1)
            def _():
                act(wcopy(0, right, zz, yy, j, False))
        if t % 2 == 0:
            @pl.when(z > 0)
            def _():
                act(wcopy(1, left, zz, yy, j, False))

    def begin(c):
        c.start()

    def forward_chunk(t, j):
        def go():
            zz = place(t)
            wait_chunk(cid(zz, y, core), j)
            on_z(t, y, j, begin)

            @pl.when(j < CH - 1)
            def _():
                wcopy(2, across, zz, y, j, False).start()

            wcopy(3, sibling, zz, y, j, False).start()
        guard(t, go)

    def forward(t):
        @pl.loop(0, CH)
        def _(j):
            forward_chunk(t, j)

    def forward_last(t):
        def go():
            zz = place(t)
            wait_chunk(cid(zz, 1 - y, core), CH - 1)
            on_z(t, 1 - y, CH - 1, begin)
            wcopy(3, sibling, zz, 1 - y, CH - 1, False).start()
        guard(t, go)

    def forward_y(t):
        def go():
            zz = place(t)

            @pl.loop(0, CH - 1)
            def _(j):
                wait_chunk(cid(zz, 1 - y, core), j)
                wcopy(3, sibling, zz, 1 - y, j, False).start()
        guard(t, go)

    nsteps = width // NB
    res_local.wait()

    @pl.loop(0, nsteps)
    def _(n):
        cols = pl.ds(pl.multiple_of(n * NB, NB), NB)
        acc[:, cols] = obuf[:, cols].astype(jnp.float32)

    scale = HD ** (-0.5) * math.log2(math.e)
    starts = []
    for i in range(half // QT):
        t0 = pl.multiple_of(r * half + i * QT, QT)
        ks = pl.multiple_of(jnp.maximum(t0 + QT - KT, 0), QT)
        starts.append((t0, ks))
        qrow = seg_row[:, pl.ds(t0, QT)].astype(jnp.float32)
        qs = jnp.broadcast_to(qrow, (128, QT)).T[:, :1]
        ksg = seg_row[:, pl.ds(ks, KT)].astype(jnp.float32)
        qp = t0 + lax.broadcasted_iota(jnp.int32, (QT, KT), 0)
        kp = ks + lax.broadcasted_iota(jnp.int32, (QT, KT), 1)
        keep = (qs == ksg) & (kp <= qp)
        bias[i] = jnp.where(keep, jnp.float32(0.0), jnp.float32(-1e30))

    q_local.wait()
    k_local.wait()
    v_local.wait()
    k_rem.wait_recv()
    v_rem.wait_recv()

    heads = qbuf.shape[1] // HD
    per_step = heads // STEPS
    aw = per_step * HD
    group = heads // HK

    def attn_copy(g):
        cols = pl.ds(pl.multiple_of(g * aw, aw), aw)
        part = attn.at[pl.ds(pl.multiple_of(r * half, half), half), cols]
        return pltpu.make_async_remote_copy(
            src_ref=part, dst_ref=part, send_sem=a_send.at[g], recv_sem=a_recv.at[g],
            device_id=partner, device_id_type=MESH)

    @pl.loop(0, STEPS)
    def _(g):
        kcol = pl.ds(pl.multiple_of((g * per_step // group) * HD, HD), HD)
        for i, (t0, ks) in enumerate(starts):
            key = kbuf[pl.ds(ks, KT), kcol]
            val = vbuf[pl.ds(ks, KT), kcol]
            for h in range(per_step):
                hc = pl.ds(pl.multiple_of(g * aw + h * HD, HD), HD)
                qh = qbuf[i * QT:(i + 1) * QT, hc]
                s = lax.dot_general(qh, key, (((1,), (1,)), ((), ())),
                                    preferred_element_type=jnp.float32)
                s = s * scale + bias[i]
                m = jnp.max(s, axis=1, keepdims=True)
                p = jnp.exp2(s - m)
                tot = jnp.sum(p, axis=1, keepdims=True)
                o = jnp.dot(p.astype(jnp.bfloat16), val, preferred_element_type=jnp.float32)
                attn[pl.ds(t0, QT), hc] = (o / tot).astype(jnp.bfloat16)
        attn_copy(g).start()
        for t in (1, 2):
            forward_chunk(t, g)


    def project(t, yy):
        def go():
            zz = place(t)

            @pl.loop(0, CH)
            def _(j):
                wait_chunk(cid(zz, yy, 1 - core), j)

            first = cid(zz, yy, 0)

            def wload(n, c):
                cols = pl.ds(pl.multiple_of(n * NB, NB), NB)
                return pltpu.make_async_copy(
                    wfull.at[first + c, :, cols], wbuf.at[pl.ds(c * wrows, wrows), cols],
                    lw.at[c, n])

            @pl.loop(0, nsteps)
            def _(n):
                wload(n, 0).start()
                wload(n, 1).start()

            kc = pl.ds(pl.multiple_of(first * wrows, 2 * wrows), 2 * wrows)

            @pl.loop(0, nsteps)
            def _(n):
                cols = pl.ds(pl.multiple_of(n * NB, NB), NB)
                wload(n, 0).wait()
                wload(n, 1).wait()
                acc[:, cols] += jnp.dot(attn[:, kc], wbuf[:, cols],
                                        preferred_element_type=jnp.float32)
        guard(t, go)

    forward_last(0)
    own_w.wait()
    forward_y(0)
    forward_last(1)
    forward_last(2)
    forward(3)
    forward(4)
    forward_last(3)
    forward_last(4)

    @pl.loop(0, STEPS)
    def _(g):
        attn_copy(g).wait_send()
        cols = pl.ds(pl.multiple_of(g * aw, aw), aw)
        part = attn.at[pl.ds(pl.multiple_of((1 - r) * half, half), half), cols]
        pltpu.make_async_copy(part, part, a_recv.at[g]).wait()

    project(0, y)
    project(1, y)
    project(2, y)
    forward(5)
    forward(6)
    forward_last(5)
    forward_last(6)
    project(0, 1 - y)
    forward_y(1)
    forward_y(2)
    project(3, y)
    project(4, y)
    project(1, 1 - y)
    project(2, 1 - y)
    forward_y(3)
    forward_y(4)
    project(5, y)
    project(6, y)
    project(3, 1 - y)
    project(4, 1 - y)
    forward_y(5)
    forward_y(6)
    project(5, 1 - y)
    project(6, 1 - y)

    def out_copy(n):
        cols = pl.ds(pl.multiple_of(n * NB, NB), NB)
        return pltpu.make_async_copy(obuf.at[:, cols], hid_ref.at[:, cols], osem.at[n])

    def finish(n, part):
        cols = pl.ds(pl.multiple_of(n * NB, NB), NB)
        a = acc[:, cols]
        obuf[:, cols] = a.astype(jnp.bfloat16)
        out_copy(n).start()
        sqr = a * a
        for i in range(NB // 128):
            part = part + sqr[:, i * 128:(i + 1) * 128]
        return part

    part = lax.fori_loop(0, nsteps, finish, jnp.zeros((acc.shape[0], 128), jnp.float32))
    sqbuf[0] = jnp.sum(part.T, axis=0, keepdims=True)
    x_sq = pltpu.make_async_remote_copy(
        src_ref=sqbuf.at[0], dst_ref=sqbuf.at[1], send_sem=x_send.at[2], recv_sem=x_recv.at[2],
        device_id=partner, device_id_type=MESH)
    x_sq.start()

    k_rem.wait_send()
    v_rem.wait_send()
    for t in range(2 * NZ - 1):
        def sent(t=t):
            zz = place(t)

            def ended(c):
                c.wait_send()

            @pl.loop(0, CH)
            def _(j):
                on_z(t, y, j, ended)
                wcopy(3, sibling, zz, y, j, False).wait_send()
                wcopy(3, sibling, zz, 1 - y, j, False).wait_send()

            @pl.loop(0, CH - 1 if t else CH)
            def _(j):
                wcopy(2, across, zz, y, j, False).wait_send()

            on_z(t, 1 - y, CH - 1, ended)
        guard(t, sent)

    @pl.loop(0, nsteps)
    def _(n):
        out_copy(n).wait()

    x_sq.wait()
    sq_ref[...] = sqbuf[0] + sqbuf[1]


def norm_kernel(hid_ref, sq_ref, gain_ref, sum_ref, out_ref):
    rows, width = hid_ref.shape
    scaled = lax.rsqrt(sq_ref[...] / D + jnp.float32(1e-05))
    column = jnp.broadcast_to(scaled, (128, rows)).T[:, :1]
    for n in range(width // NB):
        cols = slice(n * NB, (n + 1) * NB)
        hid = hid_ref[:, cols]
        sum_ref[:, cols] = hid
        out_ref[:, cols] = (hid.astype(jnp.float32) * column * gain_ref[:, cols]).astype(jnp.bfloat16)


def body_fused(query_proj, key_proj, value_proj, segment_ids, out_weight, residual, norm_gain):
    half, qw = query_proj.shape
    length = segment_ids.shape[1]
    wrows, width = out_weight.shape
    cols = lax.axis_size("col")
    hbm = pl.BlockSpec(memory_space=pl.ANY)
    vmem = pl.BlockSpec(memory_space=pltpu.VMEM)
    dma = pltpu.SemaphoreType.DMA
    hidden, squares, _ = pl.pallas_call(
        fused_kernel,
        out_shape=(
            jax.ShapeDtypeStruct((length, width), jnp.bfloat16),
            jax.ShapeDtypeStruct((1, length), jnp.float32),
            jax.ShapeDtypeStruct((cols, wrows, width), jnp.bfloat16),
        ),
        in_specs=[hbm, hbm, hbm, vmem, hbm, hbm],
        out_specs=(hbm, vmem, hbm),
        scratch_shapes=[
            pltpu.VMEM((half, qw), jnp.bfloat16),
            pltpu.VMEM((length, HK * HD), jnp.bfloat16),
            pltpu.VMEM((length, HK * HD), jnp.bfloat16),
            pltpu.VMEM((half // QT, QT, KT), jnp.float32),
            pltpu.VMEM((length, qw), jnp.bfloat16),
            pltpu.VMEM((2 * wrows, width), jnp.bfloat16),
            pltpu.VMEM((length, width), jnp.bfloat16),
            pltpu.VMEM((length, width), jnp.float32),
            pltpu.VMEM((2, 1, length), jnp.float32),
            dma((4, cols // 2, CH)),
            dma((cols, CH)),
            dma((5,)),
            dma((2, width // NB)),
            dma((STEPS,)),
            dma((STEPS,)),
            dma((3,)),
            dma((3,)),
            dma((width // NB,)),
        ],
        compiler_params=pltpu.CompilerParams(
            collective_id=0, has_side_effects=True, vmem_limit_bytes=60 * 1024 * 1024),
        name="fused",
    )(query_proj, key_proj, value_proj, segment_ids,
      out_weight, residual)
    rows = 128
    tile = pl.BlockSpec((rows, width), lambda i: (i, 0))
    return tuple(pl.pallas_call(
        norm_kernel,
        grid=(length // rows,),
        out_shape=(jax.ShapeDtypeStruct((length, width), jnp.bfloat16),) * 2,
        in_specs=[tile, pl.BlockSpec((1, rows), lambda i: (0, i)),
                  pl.BlockSpec((1, width), lambda i: (0, 0))],
        out_specs=(tile, tile),
        compiler_params=pltpu.CompilerParams(vmem_limit_bytes=32 * 1024 * 1024),
        name="norm",
    )(hidden, squares, norm_gain.reshape(1, width)))


def solution(mesh):
    placed = (
        P(("col", "row"), None),
        P(("col", "row"), None),
        P(("col", "row"), None),
        P("col", None),
        P("col", "row"),
        P("col", "row"),
        P("row"),
    )
    known = mesh.shape["row"] == 2 and mesh.shape["col"] == 4 * NZ
    return jax.shard_map(
        body_fused if known else body_any,
        mesh=mesh,
        in_specs=placed,
        out_specs=(P("col", "row"), P("col", "row")),
        check_vma=False,
    )
```

```python
import functools
import math

import jax
import jax.numpy as jnp
from jax import lax
from jax.experimental import pallas as pl
from jax.experimental.pallas import tpu as pltpu
from jax.sharding import PartitionSpec as P

D = 8192
HD = 128
HK = 4
MESH = pl.DeviceIdType.MESH


def attend_local(query_heads, key_heads, value_heads, segment_row):
    length = query_heads.shape[0]
    kv_local = key_heads.shape[1] // HD
    group = query_heads.shape[1] // HD // kv_local
    query_grid = query_heads.reshape(length, kv_local, group, HD).transpose(1, 2, 0, 3)
    key_grid = key_heads.reshape(length, kv_local, HD).transpose(1, 0, 2)
    value_grid = value_heads.reshape(length, kv_local, HD).transpose(1, 0, 2)
    places = jnp.arange(length)
    allowed = (segment_row[:, None] == segment_row[None, :]) & (places[None, :] <= places[:, None])

    def one_group(operands):
        group_query, group_key, group_value = operands
        scores = jnp.einsum(
            "gqd,kd->gqk", group_query, group_key, preferred_element_type=jnp.float32
        ) * HD ** (-0.5)
        scores = jnp.where(allowed, scores, jnp.float32(-1e30))
        peak = jnp.max(scores, axis=-1, keepdims=True)
        weights = jnp.where(allowed, jnp.exp(scores - peak), jnp.float32(0.0))
        totals = jnp.sum(weights, axis=-1, keepdims=True)
        probs = weights.astype(jnp.bfloat16)
        mixture = (
            jnp.einsum("gqk,kd->gqd", probs, group_value, preferred_element_type=jnp.float32)
            / totals
        )
        return mixture.astype(jnp.bfloat16)

    heads_out = lax.map(one_group, (query_grid, key_grid, value_grid))
    return heads_out.transpose(2, 0, 1, 3).reshape(length, kv_local * group * HD)


def widen_heads(proj_rows, repeat):
    rows_local = proj_rows.shape[0]
    kv_count = proj_rows.shape[1] // HD
    if repeat == 1:
        return proj_rows
    spread = jnp.broadcast_to(
        proj_rows.reshape(rows_local, kv_count, 1, HD), (rows_local, kv_count, repeat, HD)
    )
    return spread.reshape(rows_local, kv_count * repeat * HD)


def body_any(query_proj, key_proj, value_proj, segment_ids, out_weight, residual, norm_gain):
    row_count = lax.axis_size("row")
    repeat = max(row_count // HK, 1)
    key_wide = widen_heads(key_proj, repeat)
    value_wide = widen_heads(value_proj, repeat)
    query_heads, key_heads, value_heads = (
        lax.all_to_all(query_proj, "row", split_axis=1, concat_axis=0, tiled=True),
        lax.all_to_all(key_wide, "row", split_axis=1, concat_axis=0, tiled=True),
        lax.all_to_all(value_wide, "row", split_axis=1, concat_axis=0, tiled=True),
    )
    attn = attend_local(query_heads, key_heads, value_heads, segment_ids[0])
    panel_rows = lax.all_gather(attn, "row", axis=1, tiled=True)
    projected = jnp.dot(
        panel_rows,
        lax.all_gather(out_weight, "col", axis=0, tiled=True),
        preferred_element_type=jnp.float32,
    )
    hidden_sum = residual.astype(jnp.float32) + projected
    squares = lax.psum(jnp.sum(hidden_sum * hidden_sum, axis=1), "row")
    scaled = lax.rsqrt(squares / D + jnp.float32(1e-05))
    normed = hidden_sum * scaled[:, None] * norm_gain[None, :]
    return (hidden_sum.astype(jnp.bfloat16), normed.astype(jnp.bfloat16))


NZ = 4
CH = 8
QT = 256
KT = 768
STEPS = 8
NB = 512


def fused_kernel(q_ref, k_ref, v_ref, seg_row, w_ref, res_ref,
                 hid_ref, sq_ref, wfull,
                 qbuf, kbuf, vbuf, bias, attn, wbuf, obuf, acc, sqbuf,
                 send, recv, loc, lw, a_send, a_recv, x_send, x_recv, osem):
    r = lax.axis_index("row")
    col = lax.axis_index("col")
    core = lax.rem(col, 2)
    y = lax.rem(col // 2, 2)
    z = col // 4
    half = q_ref.shape[0]
    wrows = w_ref.shape[0]
    crow = wrows // CH
    width = w_ref.shape[1]

    def cid(zz, yy, cc):
        return (zz * 2 + yy) * 2 + cc

    right = (r, cid(z + 1, y, core))
    left = (r, cid(z - 1, y, core))
    across = (r, cid(z, 1 - y, core))
    sibling = (r, cid(z, y, 1 - core))
    partner = (1 - r, col)

    barrier = pltpu.get_barrier_semaphore()

    def greet(dev):
        pl.semaphore_signal(barrier, inc=1, device_id=dev, device_id_type=MESH)

    greet(across)
    greet(sibling)
    greet(partner)

    @pl.when(z > 0)
    def _():
        greet(left)

    @pl.when(z < NZ - 1)
    def _():
        greet(right)

    at_end = (z == 0) | (z == NZ - 1)

    @pl.when(at_end)
    def _():
        pl.semaphore_wait(barrier, 4)

    @pl.when(jnp.logical_not(at_end))
    def _():
        pl.semaphore_wait(barrier, 5)

    def wcopy(way, dev, zz, yy, j, own):
        slot = cid(zz, yy, core)
        rows = pl.ds(j * crow, crow)
        src = w_ref.at[rows, :] if own else wfull.at[slot, rows, :]
        return pltpu.make_async_remote_copy(
            src_ref=src, dst_ref=wfull.at[slot, rows, :],
            send_sem=send.at[way, zz * 2 + yy, j], recv_sem=recv.at[slot, j],
            device_id=dev, device_id_type=MESH)

    def wait_chunk(slot, j):
        rows = pl.ds(j * crow, crow)
        pltpu.make_async_copy(wfull.at[slot, rows, :], wfull.at[slot, rows, :], recv.at[slot, j]).wait()

    own_w = pltpu.make_async_copy(w_ref, wfull.at[col], loc.at[0])
    k_local = pltpu.make_async_copy(k_ref, kbuf.at[pl.ds(r * half, half), :], loc.at[1])
    v_local = pltpu.make_async_copy(v_ref, vbuf.at[pl.ds(r * half, half), :], loc.at[2])
    q_local = pltpu.make_async_copy(q_ref, qbuf, loc.at[3])
    res_local = pltpu.make_async_copy(res_ref, obuf, loc.at[4])

    def kv_remote(src, dst, i):
        return pltpu.make_async_remote_copy(
            src_ref=src, dst_ref=dst.at[pl.ds(r * half, half), :],
            send_sem=x_send.at[i], recv_sem=x_recv.at[i],
            device_id=partner, device_id_type=MESH)

    k_rem = kv_remote(k_ref, kbuf, 0)
    v_rem = kv_remote(v_ref, vbuf, 1)
    k_rem.start()
    v_rem.start()
    wcopy(2, across, z, y, CH - 1, True).start()
    for j in range(CH):
        @pl.when(z < NZ - 1)
        def _():
            wcopy(0, right, z, y, j, True).start()

        @pl.when(z > 0)
        def _():
            wcopy(1, left, z, y, j, True).start()

        if j < CH - 1:
            wcopy(2, across, z, y, j, True).start()
    k_local.start()
    v_local.start()
    q_local.start()
    res_local.start()
    own_w.start()
    for j in range(CH):
        wcopy(3, sibling, z, y, j, True).start()

    def place(t):
        h = (t + 1) // 2
        return z - h if t % 2 == 1 else z + h

    def guard(t, f):
        if t == 0:
            f()
        elif t % 2 == 1:
            pl.when(place(t) >= 0)(f)
        else:
            pl.when(place(t) < NZ)(f)

    def on_z(t, yy, j, act):
        zz = place(t)
        if t % 2 == 1 or t == 0:
            @pl.when(z < NZ - 1)
            def _():
                act(wcopy(0, right, zz, yy, j, False))
        if t % 2 == 0:
            @pl.when(z > 0)
            def _():
                act(wcopy(1, left, zz, yy, j, False))

    def begin(c):
        c.start()

    def forward_chunk(t, j):
        def go():
            zz = place(t)
            wait_chunk(cid(zz, y, core), j)
            on_z(t, y, j, begin)

            @pl.when(j < CH - 1)
            def _():
                wcopy(2, across, zz, y, j, False).start()

            wcopy(3, sibling, zz, y, j, False).start()
        guard(t, go)

    def forward(t):
        @pl.loop(0, CH)
        def _(j):
            forward_chunk(t, j)

    def forward_last(t):
        def go():
            zz = place(t)
            wait_chunk(cid(zz, 1 - y, core), CH - 1)
            on_z(t, 1 - y, CH - 1, begin)
            wcopy(3, sibling, zz, 1 - y, CH - 1, False).start()
        guard(t, go)

    def forward_y(t):
        def go():
            zz = place(t)

            @pl.loop(0, CH - 1)
            def _(j):
                wait_chunk(cid(zz, 1 - y, core), j)
                wcopy(3, sibling, zz, 1 - y, j, False).start()
        guard(t, go)

    nsteps = width // NB
    res_local.wait()

    @pl.loop(0, nsteps)
    def _(n):
        cols = pl.ds(pl.multiple_of(n * NB, NB), NB)
        acc[:, cols] = obuf[:, cols].astype(jnp.float32)

    scale = HD ** (-0.5) * math.log2(math.e)
    starts = []
    for i in range(half // QT):
        t0 = pl.multiple_of(r * half + i * QT, QT)
        ks = pl.multiple_of(jnp.maximum(t0 + QT - KT, 0), QT)
        starts.append((t0, ks))
        qrow = seg_row[:, pl.ds(t0, QT)].astype(jnp.float32)
        qs = jnp.broadcast_to(qrow, (128, QT)).T[:, :1]
        ksg = seg_row[:, pl.ds(ks, KT)].astype(jnp.float32)
        qp = t0 + lax.broadcasted_iota(jnp.int32, (QT, KT), 0)
        kp = ks + lax.broadcasted_iota(jnp.int32, (QT, KT), 1)
        keep = (qs == ksg) & (kp <= qp)
        bias[i] = jnp.where(keep, jnp.float32(0.0), jnp.float32(-1e30))

    q_local.wait()
    k_local.wait()
    v_local.wait()
    k_rem.wait_recv()
    v_rem.wait_recv()

    heads = qbuf.shape[1] // HD
    per_step = heads // STEPS
    aw = per_step * HD
    group = heads // HK

    def attn_copy(g):
        cols = pl.ds(pl.multiple_of(g * aw, aw), aw)
        part = attn.at[pl.ds(pl.multiple_of(r * half, half), half), cols]
        return pltpu.make_async_remote_copy(
            src_ref=part, dst_ref=part, send_sem=a_send.at[g], recv_sem=a_recv.at[g],
            device_id=partner, device_id_type=MESH)

    @pl.loop(0, STEPS)
    def _(step):
        toward = 1 - 2 * (z // 2)
        g = lax.rem(z + NZ + toward * (step // 2), NZ) * 2 + lax.rem(step, 2)
        kcol = pl.ds(pl.multiple_of((g * per_step // group) * HD, HD), HD)
        for i, (t0, ks) in enumerate(starts):
            key = kbuf[pl.ds(ks, KT), kcol]
            val = vbuf[pl.ds(ks, KT), kcol]
            for h in range(per_step):
                hc = pl.ds(pl.multiple_of(g * aw + h * HD, HD), HD)
                qh = qbuf[i * QT:(i + 1) * QT, hc]
                s = lax.dot_general(qh, key, (((1,), (1,)), ((), ())),
                                    preferred_element_type=jnp.float32)
                s = s * scale + bias[i]
                m = jnp.max(s, axis=1, keepdims=True)
                p = jnp.exp2(s - m)
                tot = jnp.sum(p, axis=1, keepdims=True)
                o = jnp.dot(p.astype(jnp.bfloat16), val, preferred_element_type=jnp.float32)
                attn[pl.ds(t0, QT), hc] = (o / tot).astype(jnp.bfloat16)
        attn_copy(g).start()
        for t in (1, 2):
            forward_chunk(t, step)


    def project(t, yy):
        def go():
            zz = place(t)

            @pl.loop(0, CH)
            def _(j):
                wait_chunk(cid(zz, yy, 1 - core), j)

            first = cid(zz, yy, 0)

            def wload(n, c):
                cols = pl.ds(pl.multiple_of(n * NB, NB), NB)
                return pltpu.make_async_copy(
                    wfull.at[first + c, :, cols], wbuf.at[pl.ds(c * wrows, wrows), cols],
                    lw.at[c, n])

            @pl.loop(0, nsteps)
            def _(n):
                wload(n, 0).start()
                wload(n, 1).start()

            kc = pl.ds(pl.multiple_of(first * wrows, 2 * wrows), 2 * wrows)
            g = zz * 2 + yy
            attn_copy(g).wait_send()
            part = attn.at[pl.ds(pl.multiple_of((1 - r) * half, half), half), kc]
            pltpu.make_async_copy(part, part, a_recv.at[g]).wait()

            @pl.loop(0, nsteps)
            def _(n):
                cols = pl.ds(pl.multiple_of(n * NB, NB), NB)
                wload(n, 0).wait()
                wload(n, 1).wait()
                acc[:, cols] += jnp.dot(attn[:, kc], wbuf[:, cols],
                                        preferred_element_type=jnp.float32)
        guard(t, go)

    forward_last(0)
    own_w.wait()
    forward_y(0)
    forward_last(1)
    forward_last(2)
    project(0, y)
    project(0, 1 - y)
    forward(3)
    forward(4)
    forward_last(3)
    forward_last(4)
    project(1, y)
    project(2, y)
    forward(5)
    forward(6)
    forward_last(5)
    forward_last(6)
    forward_y(1)
    forward_y(2)
    project(3, y)
    project(4, y)
    project(1, 1 - y)
    project(2, 1 - y)
    forward_y(3)
    forward_y(4)
    project(5, y)
    project(6, y)
    project(3, 1 - y)
    project(4, 1 - y)
    forward_y(5)
    forward_y(6)
    project(5, 1 - y)
    project(6, 1 - y)

    def out_copy(n):
        cols = pl.ds(pl.multiple_of(n * NB, NB), NB)
        return pltpu.make_async_copy(obuf.at[:, cols], hid_ref.at[:, cols], osem.at[n])

    def finish(n, part):
        cols = pl.ds(pl.multiple_of(n * NB, NB), NB)
        a = acc[:, cols]
        obuf[:, cols] = a.astype(jnp.bfloat16)
        out_copy(n).start()
        sqr = a * a
        for i in range(NB // 128):
            part = part + sqr[:, i * 128:(i + 1) * 128]
        return part

    part = lax.fori_loop(0, nsteps, finish, jnp.zeros((acc.shape[0], 128), jnp.float32))
    sqbuf[0] = jnp.sum(part.T, axis=0, keepdims=True)
    x_sq = pltpu.make_async_remote_copy(
        src_ref=sqbuf.at[0], dst_ref=sqbuf.at[1], send_sem=x_send.at[2], recv_sem=x_recv.at[2],
        device_id=partner, device_id_type=MESH)
    x_sq.start()

    k_rem.wait_send()
    v_rem.wait_send()
    for t in range(2 * NZ - 1):
        def sent(t=t):
            zz = place(t)

            def ended(c):
                c.wait_send()

            @pl.loop(0, CH)
            def _(j):
                on_z(t, y, j, ended)
                wcopy(3, sibling, zz, y, j, False).wait_send()
                wcopy(3, sibling, zz, 1 - y, j, False).wait_send()

            @pl.loop(0, CH - 1 if t else CH)
            def _(j):
                wcopy(2, across, zz, y, j, False).wait_send()

            on_z(t, 1 - y, CH - 1, ended)
        guard(t, sent)

    @pl.loop(0, nsteps)
    def _(n):
        out_copy(n).wait()

    x_sq.wait()
    sq_ref[...] = sqbuf[0] + sqbuf[1]


def norm_kernel(hid_ref, sq_ref, gain_ref, sum_ref, out_ref):
    rows, width = hid_ref.shape
    scaled = lax.rsqrt(sq_ref[...] / D + jnp.float32(1e-05))
    column = jnp.broadcast_to(scaled, (128, rows)).T[:, :1]
    for n in range(width // NB):
        cols = slice(n * NB, (n + 1) * NB)
        hid = hid_ref[:, cols]
        sum_ref[:, cols] = hid
        out_ref[:, cols] = (hid.astype(jnp.float32) * column * gain_ref[:, cols]).astype(jnp.bfloat16)


def body_fused(query_proj, key_proj, value_proj, segment_ids, out_weight, residual, norm_gain):
    half, qw = query_proj.shape
    length = segment_ids.shape[1]
    wrows, width = out_weight.shape
    cols = lax.axis_size("col")
    hbm = pl.BlockSpec(memory_space=pl.ANY)
    vmem = pl.BlockSpec(memory_space=pltpu.VMEM)
    dma = pltpu.SemaphoreType.DMA
    hidden, squares, _ = pl.pallas_call(
        fused_kernel,
        out_shape=(
            jax.ShapeDtypeStruct((length, width), jnp.bfloat16),
            jax.ShapeDtypeStruct((1, length), jnp.float32),
            jax.ShapeDtypeStruct((cols, wrows, width), jnp.bfloat16),
        ),
        in_specs=[hbm, hbm, hbm, vmem, hbm, hbm],
        out_specs=(hbm, vmem, hbm),
        scratch_shapes=[
            pltpu.VMEM((half, qw), jnp.bfloat16),
            pltpu.VMEM((length, HK * HD), jnp.bfloat16),
            pltpu.VMEM((length, HK * HD), jnp.bfloat16),
            pltpu.VMEM((half // QT, QT, KT), jnp.float32),
            pltpu.VMEM((length, qw), jnp.bfloat16),
            pltpu.VMEM((2 * wrows, width), jnp.bfloat16),
            pltpu.VMEM((length, width), jnp.bfloat16),
            pltpu.VMEM((length, width), jnp.float32),
            pltpu.VMEM((2, 1, length), jnp.float32),
            dma((4, cols // 2, CH)),
            dma((cols, CH)),
            dma((5,)),
            dma((2, width // NB)),
            dma((STEPS,)),
            dma((STEPS,)),
            dma((3,)),
            dma((3,)),
            dma((width // NB,)),
        ],
        compiler_params=pltpu.CompilerParams(
            collective_id=0, has_side_effects=True, vmem_limit_bytes=60 * 1024 * 1024),
        name="fused",
    )(query_proj, key_proj, value_proj, segment_ids,
      out_weight, residual)
    rows = 128
    tile = pl.BlockSpec((rows, width), lambda i: (i, 0))
    return tuple(pl.pallas_call(
        norm_kernel,
        grid=(length // rows,),
        out_shape=(jax.ShapeDtypeStruct((length, width), jnp.bfloat16),) * 2,
        in_specs=[tile, pl.BlockSpec((1, rows), lambda i: (0, i)),
                  pl.BlockSpec((1, width), lambda i: (0, 0))],
        out_specs=(tile, tile),
        compiler_params=pltpu.CompilerParams(vmem_limit_bytes=32 * 1024 * 1024),
        name="norm",
    )(hidden, squares, norm_gain.reshape(1, width)))


def solution(mesh):
    placed = (
        P(("col", "row"), None),
        P(("col", "row"), None),
        P(("col", "row"), None),
        P("col", None),
        P("col", "row"),
        P("col", "row"),
        P("row"),
    )
    known = mesh.shape["row"] == 2 and mesh.shape["col"] == 4 * NZ
    return jax.shard_map(
        body_fused if known else body_any,
        mesh=mesh,
        in_specs=placed,
        out_specs=(P("col", "row"), P("col", "row")),
        check_vma=False,
    )
```
